32 devices in a mesh: tm: 8 (over z, x), space: 4 (over y, core).
Axes of the slice: x: 2, y: 2, z: 4, core: 2. Of those that a mesh axis runs over, the one named last changes fastest.
Arguments:
- states: float32 [8, 2, 64, 256], P('tm', None, 'space'), may hold values from -6 to 6
- vel_x: int32 [64, 256], replicated, may hold values from -15 to 15
- vel_y: int32 [64, 256], replicated, may hold values from -15 to 15
- diffus: int32 [64, 256], replicated, may hold values from 1 to 10
Outputs:
- corrected: float32 [8, 2, 64, 256], P('tm', None, 'space')
- advanced: float32 [8, 2, 64, 256], P('tm', None, 'space')
- residual: float32 [8, 2, 64, 256], P('tm', None, 'space')
The draws below stay inside these ranges and needn't reach their ends.
All inputs are finite; a program needn't handle non-finite values.
Results may differ from the reference program's by a relative error of at most 0.00002.
Values sent between devices are 32-bit elements; how exact they have to be, the bound alone decides.
A program may use at most 64 MiB of HBM per device.

```python
import jax
import jax.numpy as jnp
from jax import lax

COLS = 256
STEPS = 16
NX = 64
INTERVALS = 8


def plant(values, stream_key, smallest, largest):
    spot = [jax.random.randint(jax.random.fold_in(stream_key, axis), (), 0, length) for axis, length in enumerate(values.shape)]
    main_axis = values.shape.index(max(values.shape))
    neighbour = spot[:main_axis] + [(spot[main_axis] + 1) % values.shape[main_axis]] + spot[main_axis + 1:]
    return values.at[tuple(spot)].set(smallest).at[tuple(neighbour)].set(largest)


def block_scale(rng, shape, split, low, largest):
    gain, own = 1.0, jax.random.fold_in(rng, 6)
    for axis_at, shards_of in split:
        draws = jnp.exp(jax.random.uniform(jax.random.fold_in(own, axis_at), (shards_of,), jnp.float32, low / len(split), largest / len(split)))
        gain = gain * jnp.repeat(draws, shape[axis_at] // shards_of).reshape([-1 if axis == axis_at else 1 for axis in range(len(shape))])
    return gain


def noise(rng, extent, deviation, reach, shards=(), held_as=jnp.bfloat16):
    drawn = deviation * jax.random.normal(rng, extent, jnp.float32)
    if shards:
        drawn = drawn * block_scale(rng, extent, shards, -0.22, 0.18)
    return jnp.clip(drawn, -reach, reach).astype(held_as)


def setup_inputs(seed: int = 0) -> dict:
    arg_keys = jax.random.split(jax.random.key(seed), 5)
    return {
        "states": noise(arg_keys[0], (INTERVALS, 2, NX, COLS), 1.0, 6.0, ((0, 8), (2, 4)), jnp.float32),
        "vel_x": plant(jax.random.randint(arg_keys[1], (NX, COLS), -15, 16), jax.random.fold_in(arg_keys[1], 1), -15, 15).astype(jnp.int32),
        "vel_y": plant(jax.random.randint(arg_keys[2], (NX, COLS), -15, 16), jax.random.fold_in(arg_keys[2], 1), -15, 15).astype(jnp.int32),
        "diffus": plant(jax.random.randint(arg_keys[3], (NX, COLS), 1, 11), jax.random.fold_in(arg_keys[3], 1), 1, 10).astype(jnp.int32),
    }


def tracer_scales():
    return jnp.array([1.0, 0.5], jnp.float32)[:, None, None]


def coefficients(vel_x, vel_y, diffus):
    return (0.01 * vel_x.astype(jnp.float32), 0.01 * vel_y.astype(jnp.float32), 0.005 * diffus.astype(jnp.float32))


def advance(field, coefs, factor):
    courant_x, courant_y, diffusion = coefs
    widths = ((0, 0),) * (field.ndim - 2) + ((1, 1), (1, 1))
    padded = jnp.pad(field, widths)
    row_above = padded[..., :-2, 1:-1]
    row_below = padded[..., 2:, 1:-1]
    column_left = padded[..., 1:-1, :-2]
    column_right = padded[..., 1:-1, 2:]
    transport = (jnp.maximum(courant_x, 0.0) * (field - row_above) + jnp.minimum(courant_x, 0.0) * (row_below - field)
                 + jnp.maximum(courant_y, 0.0) * (field - column_left) + jnp.minimum(courant_y, 0.0) * (column_right - field))
    laplace = row_above + row_below + column_left + column_right - 4.0 * field
    return field + factor * (diffusion * tracer_scales() * laplace - transport)


def propagate(field, count, factor, coefs):
    return lax.fori_loop(0, count, lambda turn_index, current: advance(current, coefs, factor), field)


def reference(states, vel_x, vel_y, diffus):
    coefs = coefficients(vel_x, vel_y, diffus)
    interval_ends = propagate(states, STEPS, 1.0, coefs)
    starts = jnp.concatenate([states[:1], interval_ends[:-1]], 0)
    second_ends = propagate(starts, STEPS, 1.0, coefs)
    coarse_starts = propagate(starts, STEPS // 2, 2.0, coefs)
    residual = jnp.concatenate([jnp.zeros_like(states[:1]), second_ends[:-1] - starts[1:]], 0)
    forcing = jnp.concatenate([states[:1], second_ends[:-1] - coarse_starts[:-1]], 0)

    def coarse_turn(carried, forcing_slot):
        updated = propagate(carried, STEPS // 2, 2.0, coefs) + forcing_slot
        return updated, updated

    _, corrected = lax.scan(coarse_turn, jnp.zeros(states.shape[1:], jnp.float32), forcing)
    advanced = propagate(corrected, STEPS, 1.0, coefs)
    return corrected, advanced, residual
```

```python
import functools

import jax
import jax.numpy as jnp
from jax import lax
from jax.experimental import pallas as pl
from jax.experimental.pallas import tpu as pltpu
from jax.sharding import PartitionSpec as P

STEPS = 16
COARSE = STEPS // 2
LANES = 128
SUB = 8
MESH = pl.DeviceIdType.MESH


def load(ref, stacks, tiles):
    return [[ref[k, :, w * LANES : (w + 1) * LANES] for w in range(tiles)] for k in range(stacks)]


def load_rows(ref, stacks, tiles):
    return [[ref[w, pl.ds(k, SUB, stride=stacks), :] for w in range(tiles)] for k in range(stacks)]


def store(ref, u):
    for k, row in enumerate(u):
        for w, value in enumerate(row):
            ref[k, :, w * LANES : (w + 1) * LANES] = value


def store_rows(ref, u):
    stacks = len(u)
    for k, row in enumerate(u):
        for w, value in enumerate(row):
            ref[w, pl.ds(k, SUB, stride=stacks), :] = value


def each(f, *fields):
    return [[f(*values) for values in zip(*rows)] for rows in zip(*fields)]


def advance(fields, coefs):
    stacks, tiles = len(fields[0]), len(fields[0][0])
    lane = lax.broadcasted_iota(jnp.int32, (SUB, LANES), 1)
    first, last = lane == 0, lane == LANES - 1
    out = [[[None] * tiles for _ in range(stacks)] for _ in fields]
    tops = [[pltpu.roll(u[stacks - 1][w], 1, 0) for w in range(tiles)] for u in fields]
    bottoms = [[pltpu.roll(u[0][w], SUB - 1, 0) for w in range(tiles)] for u in fields]
    for k in range(stacks):
        c = [[coefs[i, k, :, w * LANES : (w + 1) * LANES] for w in range(tiles)] for i in range(5)]
        for f, u in enumerate(fields):
            right = [pltpu.roll(v, 1, 1) for v in u[k]]
            left = [pltpu.roll(v, LANES - 1, 1) for v in u[k]]
            for w in range(tiles):
                a = u[k - 1][w] if k else tops[f][w]
                b = u[k + 1][w] if k + 1 < stacks else bottoms[f][w]
                l = jnp.where(first, right[w - 1], right[w]) if w else right[w]
                r = jnp.where(last, left[w + 1], left[w]) if w + 1 < tiles else left[w]
                out[f][k][w] = (c[0][w] * u[k][w] + (c[1][w] * a + c[2][w] * b)) + (c[3][w] * l + c[4][w] * r)
    return out


def propagate(fields, coefs, count):
    return lax.fori_loop(0, count, lambda _, now: advance(now, coefs), fields)


def kernel(
    states, vel_x, vel_y, diffus, corrected, advanced, residual,
    tables, fine, coarse, gathered, starts, addends, last_residual, blocks, plain,
    table_sem, send_sem, recv_sem, block_send, block_recv, out_send, out_recv,
):
    groups, places = lax.axis_size("tm") // 2, lax.axis_size("space")
    p, s = lax.axis_index("tm"), lax.axis_index("space")
    g = lax.div(p, 2)
    x = p - 2 * g
    tracer = lax.rem(s, 2)
    partner = s + 1 - 2 * tracer
    rows = states.shape[2]
    stacks, tiles = fine.shape[1], fine.shape[3] // LANES

    def columns(w):
        return pl.ds(w * LANES, LANES)

    loads = [
        pltpu.make_async_copy(ref.at[:, columns(w)], tables.at[i, w], table_sem.at[i, w])
        for i, ref in enumerate((vel_x, vel_y, diffus))
        for w in range(tiles)
    ]
    for copy in loads:
        copy.start()

    barrier = pltpu.get_barrier_semaphore()

    def greet(pp, ss):
        pl.semaphore_signal(barrier, 1, device_id=(pp, ss), device_id_type=MESH)

    for ss in range(places):
        @pl.when((x == 1) | (s != ss))
        def _():
            greet(2 * g, ss)

        @pl.when(g > 0)
        def _():
            greet(2 * g - 2, ss)
            greet(2 * g - 1, ss)

    greet(p, partner)

    def greet_block(i, carry):
        greet(2 * i + x, s)
        return carry

    lax.fori_loop(0, g, greet_block, 0)
    ahead = groups - 1 - g
    more = jnp.where(ahead > 0, 2 * places, 0)
    pl.semaphore_wait(barrier, (1 - x) * (2 * places - 1) + more + ahead + 1)

    my_rows = pl.ds(pl.multiple_of(s * rows, SUB), rows)
    partner_rows = pl.ds(pl.multiple_of(partner * rows, SUB), rows)

    def piece(role, pp, ss, slot, w):
        return pltpu.make_async_remote_copy(
            src_ref=states.at[0, ss % 2, :, columns(w)],
            dst_ref=gathered.at[role, w, my_rows],
            send_sem=send_sem.at[slot, w],
            recv_sem=recv_sem.at[role],
            device_id=(pp, ss),
            device_id_type=MESH,
        )

    own = [
        pltpu.make_async_copy(states.at[0, tracer, :, columns(w)], gathered.at[2, w, my_rows], recv_sem.at[2])
        for w in range(tiles)
    ]

    def to_next(act):
        @pl.when(ahead > 0)
        def _():
            for m in range(2):
                for ss in range(places):
                    for w in range(tiles):
                        act(piece(x, 2 * g + 2 + m, ss, m * places + ss, w))

    def to_group(act):
        @pl.when(x == 0)
        def _():
            for ss in range(places):
                for w in range(tiles):
                    act(piece(2, 2 * g + 1, ss, 3 * places + ss, w))
            for ss in range(places):
                @pl.when(s != ss)
                def _():
                    for w in range(tiles):
                        act(piece(2, 2 * g, ss, 2 * places + ss, w))

    to_next(lambda copy: copy.start())
    to_group(lambda copy: copy.start())

    @pl.when(x == 0)
    def _():
        for copy in own:
            copy.start()

    @pl.when(g == 0)
    def _():
        gathered[0] = jnp.zeros(gathered.shape[1:], jnp.float32)
        gathered[1] = jnp.zeros(gathered.shape[1:], jnp.float32)

    for copy in loads:
        copy.wait()
    scale = jnp.where(tracer == 0, 1.0, 0.5).astype(jnp.float32)
    sub = lax.broadcasted_iota(jnp.int32, (SUB, LANES), 0)
    lane = lax.broadcasted_iota(jnp.int32, (SUB, LANES), 1)
    for k, w in [(k, w) for k in range(stacks) for w in range(tiles)]:
        cx, cy, d = (tables[i, w, pl.ds(k, SUB, stride=stacks), :].astype(jnp.float32) for i in range(3))
        cx, cy, d = 0.01 * cx, 0.01 * cy, (0.005 * d) * scale
        above, below = d + jnp.maximum(cx, 0.0), d - jnp.minimum(cx, 0.0)
        before, after = d + jnp.maximum(cy, 0.0), d - jnp.minimum(cy, 0.0)
        total = (above + below) + (before + after)
        if k == 0:
            above = jnp.where(sub == 0, 0.0, above)
        if k == stacks - 1:
            below = jnp.where(sub == SUB - 1, 0.0, below)
        if w == 0:
            before = jnp.where(lane == 0, 0.0, before)
        if w == tiles - 1:
            after = jnp.where(lane == LANES - 1, 0.0, after)
        for table, factor in ((fine, 1.0), (coarse, 2.0)):
            table[0, k, :, columns(w)] = 1.0 - factor * total
            for i, value in enumerate((above, below, before, after)):
                table[i + 1, k, :, columns(w)] = factor * value

    def arrive(role):
        pltpu.make_async_remote_copy(
            src_ref=gathered.at[role],
            dst_ref=gathered.at[role],
            send_sem=send_sem.at[0, 0],
            recv_sem=recv_sem.at[role],
            device_id=(p, partner),
            device_id_type=MESH,
        ).wait_recv()

    arrive(2)

    @pl.when(g > 0)
    def _():
        arrive(0)
        arrive(1)

    a0, b0, d0 = (load_rows(gathered.at[role], stacks, tiles) for role in range(3))
    a1, b1, d1 = propagate([a0, b0, d0], fine, STEPS)
    at_start = g == 0
    b1 = each(lambda u, v: jnp.where(at_start, v, u), b1, load_rows(gathered.at[2], stacks, tiles))
    store(starts.at[0], b1)
    store(starts.at[1], d1)
    a2, b2 = propagate([a1, b1], fine, STEPS)
    r0 = each(lambda u, v: jnp.where(at_start, 0.0, u - v), a2, load(starts.at[0], stacks, tiles))
    store(addends.at[0], r0)
    r1 = each(lambda u, v: u - v, b2, load(starts.at[1], stacks, tiles))
    store(last_residual, r1)
    (block,) = propagate([r0], coarse, COARSE)
    store(addends.at[1], each(lambda u, v: u + v, block, load(last_residual, stacks, tiles)))

    def block_copy(i):
        return pltpu.make_async_remote_copy(
            src_ref=addends.at[1],
            dst_ref=blocks.at[g],
            send_sem=block_send.at[i],
            recv_sem=block_recv.at[g],
            device_id=(2 * i + x, s),
            device_id_type=MESH,
        )

    def start_block(n, carry):
        block_copy(groups - 1 - n).start()
        return carry

    lax.fori_loop(0, ahead, start_block, 0)

    def hand_over(which, out, w):
        return pltpu.make_async_remote_copy(
            src_ref=plain.at[which, w, partner_rows],
            dst_ref=out.at[0, tracer, :, columns(w)],
            send_sem=out_send.at[which, w],
            recv_sem=out_recv.at[which, w],
            device_id=(p, partner),
            device_id_type=MESH,
        )

    def put(which, out, u):
        store_rows(plain.at[which], u)
        for w in range(tiles):
            hand_over(which, out, w).start()
        for w in range(tiles):
            out[0, tracer, :, columns(w)] = plain[which, w, my_rows]

    put(0, residual, each(lambda u, v: jnp.where(x == 0, u, v), load(addends.at[0], stacks, tiles), load(last_residual, stacks, tiles)))

    def take_block(i, e):
        (e,) = propagate([e], coarse, STEPS)
        pltpu.make_async_remote_copy(
            src_ref=addends.at[1],
            dst_ref=blocks.at[i],
            send_sem=block_send.at[0],
            recv_sem=block_recv.at[i],
            device_id=(p, partner),
            device_id_type=MESH,
        ).wait_recv()
        return each(lambda u, v: u + v, e, load(blocks.at[i], stacks, tiles))

    zero = [[jnp.zeros((SUB, LANES), jnp.float32)] * tiles for _ in range(stacks)]
    e = lax.fori_loop(0, g, take_block, zero)
    (e,) = propagate([e], coarse, COARSE * (1 + x))
    e = each(lambda u, v: u + v, e, load(addends.at[x], stacks, tiles))
    now = each(lambda u, v: u + v, e, load(starts.at[x], stacks, tiles))
    put(1, corrected, now)
    (now,) = propagate([now], fine, STEPS)
    put(2, advanced, now)

    to_next(lambda copy: copy.wait_send())
    to_group(lambda copy: copy.wait_send())

    def end_block(n, carry):
        block_copy(groups - 1 - n).wait_send()
        return carry

    lax.fori_loop(0, ahead, end_block, 0)
    for which, out in enumerate((residual, corrected, advanced)):
        for w in range(tiles):
            hand_over(which, out, w).wait()


def on_device(states, vel_x, vel_y, diffus):
    groups, places = lax.axis_size("tm") // 2, lax.axis_size("space")
    nx, cols = vel_x.shape
    stacks = nx // SUB
    tiles = cols // LANES
    field, grid = (stacks, SUB, cols), (tiles, nx, LANES)
    out = jax.ShapeDtypeStruct(states.shape, jnp.float32)
    return pl.pallas_call(
        kernel,
        out_shape=(out, out, out),
        in_specs=[pl.BlockSpec(memory_space=pl.ANY)] * 4,
        out_specs=(pl.BlockSpec(memory_space=pltpu.VMEM),) * 3,
        scratch_shapes=[
            pltpu.VMEM((3, *grid), jnp.int32),
            pltpu.VMEM((5, *field), jnp.float32),
            pltpu.VMEM((5, *field), jnp.float32),
            pltpu.VMEM((3, *grid), jnp.float32),
            pltpu.VMEM((2, *field), jnp.float32),
            pltpu.VMEM((2, *field), jnp.float32),
            pltpu.VMEM(field, jnp.float32),
            pltpu.VMEM((groups, *field), jnp.float32),
            pltpu.VMEM((3, *grid), jnp.float32),
            pltpu.SemaphoreType.DMA((3, tiles)),
            pltpu.SemaphoreType.DMA((4 * places, tiles)),
            pltpu.SemaphoreType.DMA((3,)),
            pltpu.SemaphoreType.DMA((groups,)),
            pltpu.SemaphoreType.DMA((groups,)),
            pltpu.SemaphoreType.DMA((3, tiles)),
            pltpu.SemaphoreType.DMA((3, tiles)),
        ],
        compiler_params=pltpu.CompilerParams(collective_id=0, has_side_effects=True),
    )(states, vel_x, vel_y, diffus)


def solution(mesh):
    split = P("tm", None, "space", None)
    return jax.shard_map(
        on_device,
        mesh=mesh,
        in_specs=(split, P(), P(), P()),
        out_specs=(split, split, split),
        check_vma=False,
    )
```

```python
import functools

import jax
import jax.numpy as jnp
from jax import lax
from jax.experimental import pallas as pl
from jax.experimental.pallas import tpu as pltpu
from jax.sharding import PartitionSpec as P

STEPS = 16
COARSE = STEPS // 2
LANES = 128
SUB = 8
MESH = pl.DeviceIdType.MESH


def load(ref, stacks, tiles):
    return [[ref[k, :, w * LANES : (w + 1) * LANES] for w in range(tiles)] for k in range(stacks)]


def load_rows(ref, stacks, tiles):
    return [[ref[w, pl.ds(k, SUB, stride=stacks), :] for w in range(tiles)] for k in range(stacks)]


def store(ref, u):
    for k, row in enumerate(u):
        for w, value in enumerate(row):
            ref[k, :, w * LANES : (w + 1) * LANES] = value


def store_rows(ref, u):
    stacks = len(u)
    for k, row in enumerate(u):
        for w, value in enumerate(row):
            ref[w, pl.ds(k, SUB, stride=stacks), :] = value


def each(f, *fields):
    return [[f(*values) for values in zip(*rows)] for rows in zip(*fields)]


def deal(u):
    tiles = len(u)
    lane = lax.broadcasted_iota(jnp.int32, (SUB, LANES), 1)
    out = []
    for w in range(tiles):
        column = tiles * lane + w
        picks = [jnp.take_along_axis(v, column % LANES, axis=1) for v in u]
        value = picks[0]
        for v in range(1, tiles):
            value = jnp.where(column >= v * LANES, picks[v], value)
        out.append(value)
    return out


def undeal(u):
    tiles = len(u)
    lane = lax.broadcasted_iota(jnp.int32, (SUB, LANES), 1)
    out = []
    for v in range(tiles):
        column = v * LANES + lane
        picks = [jnp.take_along_axis(x, column // tiles, axis=1) for x in u]
        value = picks[0]
        for w in range(1, tiles):
            value = jnp.where(column % tiles == w, picks[w], value)
        out.append(value)
    return out


def advance(fields, coefs):
    stacks, tiles = len(fields[0]), len(fields[0][0])
    out = [[[None] * tiles for _ in range(stacks)] for _ in fields]
    tops = [[pltpu.roll(u[stacks - 1][w], 1, 0) for w in range(tiles)] for u in fields]
    bottoms = [[pltpu.roll(u[0][w], SUB - 1, 0) for w in range(tiles)] for u in fields]
    for k in range(stacks):
        c = [[coefs[i, k, :, w * LANES : (w + 1) * LANES] for w in range(tiles)] for i in range(5)]
        for f, u in enumerate(fields):
            right = pltpu.roll(u[k][tiles - 1], 1, 1)
            left = pltpu.roll(u[k][0], LANES - 1, 1)
            for w in range(tiles):
                a = u[k - 1][w] if k else tops[f][w]
                b = u[k + 1][w] if k + 1 < stacks else bottoms[f][w]
                l = u[k][w - 1] if w else right
                r = u[k][w + 1] if w + 1 < tiles else left
                near = c[0][w] * u[k][w] + (c[1][w] * a + c[2][w] * b)
                if w == 0:
                    out[f][k][w] = (near + c[4][w] * r) + c[3][w] * l
                else:
                    out[f][k][w] = (near + c[3][w] * l) + c[4][w] * r
    return out


def propagate(fields, coefs, count, unroll=4):
    def turn(_, now):
        for _ in range(unroll):
            now = advance(now, coefs)
        return now

    return lax.fori_loop(0, count // unroll, turn, fields)


def kernel(
    states, vel_x, vel_y, diffus, corrected, advanced, residual,
    tables, own_block, staged, fine, coarse, gathered, starts, addends, last_residual, blocks, plain, outgoing,
    table_sem, own_sem, send_sem, recv_sem, block_send, block_recv, out_send, out_recv,
):
    groups, places = lax.axis_size("tm") // 2, lax.axis_size("space")
    p, s = lax.axis_index("tm"), lax.axis_index("space")
    g = lax.div(p, 2)
    x = p - 2 * g
    tracer = lax.rem(s, 2)
    partner = s + 1 - 2 * tracer
    rows = states.shape[2]
    stacks, tiles = fine.shape[1], fine.shape[3] // LANES

    def columns(w):
        return pl.ds(w * LANES, LANES)

    loads = [
        pltpu.make_async_copy(ref.at[:, columns(w)], tables.at[i, w], table_sem.at[i, w])
        for i, ref in enumerate((vel_x, vel_y, diffus))
        for w in range(tiles)
    ]
    own_load = pltpu.make_async_copy(states.at[0], own_block, own_sem)
    own_load.start()
    for copy in loads:
        copy.start()

    barrier = pltpu.get_barrier_semaphore()

    def greet(pp, ss):
        pl.semaphore_signal(barrier, 1, device_id=(pp, ss), device_id_type=MESH)

    for ss in range(places):
        @pl.when((x == 1) | (s != ss))
        def _():
            greet(2 * g, ss)

        @pl.when(g > 0)
        def _():
            greet(2 * g - 2, ss)
            greet(2 * g - 1, ss)

    greet(p, partner)

    def greet_block(i, carry):
        greet(2 * i + x, s)
        return carry

    lax.fori_loop(0, g, greet_block, 0)
    ahead = groups - 1 - g
    tracers = states.shape[1]
    own_load.wait()
    for t in range(tracers):
        for i in range(0, rows, SUB):
            natural = [own_block[t, i : i + SUB, columns(w)] for w in range(tiles)]
            for w, value in enumerate(deal(natural)):
                staged[t, w, i : i + SUB] = value

    more = jnp.where(ahead > 0, 2 * places, 0)
    pl.semaphore_wait(barrier, (1 - x) * (2 * places - 1) + more + ahead + 1)

    my_rows = pl.ds(pl.multiple_of(s * rows, SUB), rows)

    def piece(role, pp, ss, slot):
        return pltpu.make_async_remote_copy(
            src_ref=staged.at[ss % 2],
            dst_ref=gathered.at[role, :, my_rows],
            send_sem=send_sem.at[slot],
            recv_sem=recv_sem.at[role],
            device_id=(pp, ss),
            device_id_type=MESH,
        )

    own = pltpu.make_async_copy(staged.at[tracer], gathered.at[2, :, my_rows], recv_sem.at[2])

    def to_next(act):
        @pl.when(ahead > 0)
        def _():
            for m in range(2):
                for ss in range(places):
                    act(piece(x, 2 * g + 2 + m, ss, m * places + ss))

    def to_group(act):
        @pl.when(x == 0)
        def _():
            for ss in range(places):
                act(piece(2, 2 * g + 1, ss, 3 * places + ss))
            for ss in range(places):
                @pl.when(s != ss)
                def _():
                    act(piece(2, 2 * g, ss, 2 * places + ss))

    to_next(lambda copy: copy.start())
    to_group(lambda copy: copy.start())

    @pl.when(x == 0)
    def _():
        own.start()

    @pl.when(g == 0)
    def _():
        gathered[0] = jnp.zeros(gathered.shape[1:], jnp.float32)
        gathered[1] = jnp.zeros(gathered.shape[1:], jnp.float32)

    for copy in loads:
        copy.wait()
    scale = jnp.where(tracer == 0, 1.0, 0.5).astype(jnp.float32)
    sub = lax.broadcasted_iota(jnp.int32, (SUB, LANES), 0)
    lane = lax.broadcasted_iota(jnp.int32, (SUB, LANES), 1)
    def put_coefficients(k, w, cx, cy, d):
        cx, cy, d = 0.01 * cx, 0.01 * cy, (0.005 * d) * scale
        above, below = d + jnp.maximum(cx, 0.0), d - jnp.minimum(cx, 0.0)
        before, after = d + jnp.maximum(cy, 0.0), d - jnp.minimum(cy, 0.0)
        total = (above + below) + (before + after)
        if k == 0:
            above = jnp.where(sub == 0, 0.0, above)
        if k == stacks - 1:
            below = jnp.where(sub == SUB - 1, 0.0, below)
        if w == 0:
            before = jnp.where(lane == 0, 0.0, before)
        if w == tiles - 1:
            after = jnp.where(lane == LANES - 1, 0.0, after)
        for table, factor in ((fine, 1.0), (coarse, 2.0)):
            table[0, k, :, columns(w)] = 1.0 - factor * total
            for i, value in enumerate((above, below, before, after)):
                table[i + 1, k, :, columns(w)] = factor * value

    for k in range(stacks):
        dealt = []
        for i in range(3):
            levels = [tables[i, w, pl.ds(k, SUB, stride=stacks), :].astype(jnp.float32) for w in range(tiles)]
            dealt.append(deal(levels))
        for w in range(tiles):
            put_coefficients(k, w, *(table[w] for table in dealt))

    def arrive(role):
        pltpu.make_async_remote_copy(
            src_ref=gathered.at[role],
            dst_ref=gathered.at[role],
            send_sem=send_sem.at[0],
            recv_sem=recv_sem.at[role],
            device_id=(p, partner),
            device_id_type=MESH,
        ).wait_recv()

    arrive(2)
    first = load_rows(gathered.at[2], stacks, tiles)
    (d1,) = propagate([first], fine, STEPS)
    store(starts.at[1], d1)

    @pl.when(g > 0)
    def _():
        arrive(0)
        arrive(1)

    a0, b0 = (load_rows(gathered.at[role], stacks, tiles) for role in range(2))
    a1, b1 = propagate([a0, b0], fine, STEPS, 1)
    at_start = g == 0
    b1 = each(lambda u, v: jnp.where(at_start, v, u), b1, load_rows(gathered.at[2], stacks, tiles))
    store(starts.at[0], b1)
    a2, b2 = propagate([a1, b1], fine, STEPS, 1)
    r0 = each(lambda u, v: jnp.where(at_start, 0.0, u - v), a2, load(starts.at[0], stacks, tiles))
    store(addends.at[0], r0)
    r1 = each(lambda u, v: u - v, b2, load(starts.at[1], stacks, tiles))
    store(last_residual, r1)
    (block,) = propagate([r0], coarse, COARSE)
    store(addends.at[1], each(lambda u, v: u + v, block, load(last_residual, stacks, tiles)))

    def block_copy(i):
        return pltpu.make_async_remote_copy(
            src_ref=addends.at[1],
            dst_ref=blocks.at[g],
            send_sem=block_send.at[i],
            recv_sem=block_recv.at[g],
            device_id=(2 * i + x, s),
            device_id_type=MESH,
        )

    def start_block(n, carry):
        block_copy(groups - 1 - n).start()
        return carry

    lax.fori_loop(0, ahead, start_block, 0)

    def hand_over(which, out):
        return pltpu.make_async_remote_copy(
            src_ref=outgoing.at[which],
            dst_ref=out.at[0, tracer],
            send_sem=out_send.at[which],
            recv_sem=out_recv.at[which],
            device_id=(p, partner),
            device_id_type=MESH,
        )

    def put(which, out, u):
        store_rows(plain.at[which], u)
        for place, mine in ((partner, False), (s, True)):
            for i in range(0, rows, SUB):
                at = pl.ds(pl.multiple_of(place * rows + i, SUB), SUB)
                for w, value in enumerate(undeal([plain[which, w, at] for w in range(tiles)])):
                    if mine:
                        out[0, tracer, i : i + SUB, columns(w)] = value
                    else:
                        outgoing[which, i : i + SUB, columns(w)] = value
            if not mine:
                hand_over(which, out).start()

    put(0, residual, each(lambda u, v: jnp.where(x == 0, u, v), load(addends.at[0], stacks, tiles), load(last_residual, stacks, tiles)))

    def take_block(i, e):
        (e,) = propagate([e], coarse, STEPS)
        pltpu.make_async_remote_copy(
            src_ref=addends.at[1],
            dst_ref=blocks.at[i],
            send_sem=block_send.at[0],
            recv_sem=block_recv.at[i],
            device_id=(p, partner),
            device_id_type=MESH,
        ).wait_recv()
        return each(lambda u, v: u + v, e, load(blocks.at[i], stacks, tiles))

    zero = [[jnp.zeros((SUB, LANES), jnp.float32)] * tiles for _ in range(stacks)]
    e = lax.fori_loop(0, g, take_block, zero)
    (e,) = propagate([e], coarse, COARSE * (1 + x))
    e = each(lambda u, v: u + v, e, load(addends.at[x], stacks, tiles))
    now = each(lambda u, v: u + v, e, load(starts.at[x], stacks, tiles))
    put(1, corrected, now)
    (now,) = propagate([now], fine, STEPS)
    put(2, advanced, now)

    to_next(lambda copy: copy.wait_send())
    to_group(lambda copy: copy.wait_send())

    def end_block(n, carry):
        block_copy(groups - 1 - n).wait_send()
        return carry

    lax.fori_loop(0, ahead, end_block, 0)
    for which, out in enumerate((residual, corrected, advanced)):
        hand_over(which, out).wait()


def on_device(states, vel_x, vel_y, diffus):
    groups, places = lax.axis_size("tm") // 2, lax.axis_size("space")
    nx, cols = vel_x.shape
    stacks = nx // SUB
    tiles = cols // LANES
    field, grid = (stacks, SUB, cols), (tiles, nx, LANES)
    out = jax.ShapeDtypeStruct(states.shape, jnp.float32)
    return pl.pallas_call(
        kernel,
        out_shape=(out, out, out),
        in_specs=[pl.BlockSpec(memory_space=pl.ANY)] * 4,
        out_specs=(pl.BlockSpec(memory_space=pltpu.VMEM),) * 3,
        scratch_shapes=[
            pltpu.VMEM((3, *grid), jnp.int32),
            pltpu.VMEM(states.shape[1:], jnp.float32),
            pltpu.VMEM((states.shape[1], tiles, states.shape[2], LANES), jnp.float32),
            pltpu.VMEM((5, *field), jnp.float32),
            pltpu.VMEM((5, *field), jnp.float32),
            pltpu.VMEM((3, *grid), jnp.float32),
            pltpu.VMEM((2, *field), jnp.float32),
            pltpu.VMEM((2, *field), jnp.float32),
            pltpu.VMEM(field, jnp.float32),
            pltpu.VMEM((groups, *field), jnp.float32),
            pltpu.VMEM((3, *grid), jnp.float32),
            pltpu.VMEM((3, *states.shape[2:]), jnp.float32),
            pltpu.SemaphoreType.DMA((3, tiles)),
            pltpu.SemaphoreType.DMA(()),
            pltpu.SemaphoreType.DMA((4 * places,)),
            pltpu.SemaphoreType.DMA((3,)),
            pltpu.SemaphoreType.DMA((groups,)),
            pltpu.SemaphoreType.DMA((groups,)),
            pltpu.SemaphoreType.DMA((3,)),
            pltpu.SemaphoreType.DMA((3,)),
        ],
        compiler_params=pltpu.CompilerParams(collective_id=0, has_side_effects=True),
    )(states, vel_x, vel_y, diffus)


def solution(mesh):
    split = P("tm", None, "space", None)
    return jax.shard_map(
        on_device,
        mesh=mesh,
        in_specs=(split, P(), P(), P()),
        out_specs=(split, split, split),
        check_vma=False,
    )
```
